32 devices in a mesh: dom: 8 (over z, y), mp: 4 (over x, core).
Axes of the slice: x: 2, y: 2, z: 4, core: 2. Of those that a mesh axis runs over, the one named last changes fastest.
Arguments:
- grid_feat: bfloat16 [32768, 256], P(('dom', 'mp')), may hold values from -6 to 6
- grid_target: int32 [32768], P(('dom', 'mp')), may hold values from 0 to 8191, as said below
- enc_w1: bfloat16 [256, 512], replicated, may hold values from -0.375 to 0.375
- enc_b1: float32 [512], replicated, may hold values from -3 to 3
- enc_w2: bfloat16 [512, 512], replicated, may hold values from -0.25 to 0.25
- enc_gain: float32 [512], replicated, may hold values from 0.25 to 1.75
- mesh_embed: bfloat16 [8192, 512], P('dom', 'mp'), may hold values from -6 to 6
- nbr_blocks: int32 [128, 16], P('dom'), may hold values from 0 to 127, as said below
- attn_bias: float32 [8, 16, 8192], P('mp', None, 'dom'), may hold values from -2 to 300
- ln_gain: float32 [2, 2, 512], replicated, may hold values from 0.25 to 1.75
- qkv_w: bfloat16 [2, 3, 512, 512], P(None, None, None, 'mp'), may hold values from -0.25 to 0.25
- out_w: bfloat16 [2, 512, 512], P(None, 'mp'), may hold values from -0.25 to 0.25
- up_w: bfloat16 [2, 512, 2048], P(None, None, 'mp'), may hold values from -0.25 to 0.25
- down_w: bfloat16 [2, 2048, 512], P(None, 'mp'), may hold values from -0.125 to 0.125
Outputs:
- mesh_out: bfloat16 [8192, 512], P('dom', 'mp')
The draws below stay inside these ranges and needn't reach their ends.
Inputs may be any that keep to these rules, and one draw needn't show every extreme that they name: `grid_target`: among the 1024 grid nodes of one device (devices in the order dom, then mp), at most 256 have targets among the mesh nodes e * 1024 to (e + 1) * 1024 - 1 of one dom index e, and in every draw some dom index receives exactly 256 from every device. `nbr_blocks`: row b lists 16 different blocks, b itself among them, all within the 24 blocks that start at (b // 16) * 16 - 4, counted around the cycle of 128 blocks.
All inputs are finite; a program needn't handle non-finite values.
Results may differ from the reference program's by a relative error of at most 0.014.
Values may be sent and summed in bfloat16 or wider, within the bound.
A program may use at most 128 MiB of HBM per device.

```python
import jax
import jax.numpy as jnp
from jax import lax

D = 512
HEADS = 8
HEAD_DIM = 64
FF = 2048
F_IN = 256
LAYERS = 2
BLK = 64
NBLK = 16
HB = 4
GR_DEV = 1024
BLOCKS_DEV = 16
CAP = 256
M_DEV = 1024
MESH = 8192
BLOCKS = 128
GRID = 32768
N_DOM = 8


def draw_grid_target(key, part):
    dom_total = MESH // M_DEV
    slot_total = dom_total * CAP
    spread_top = max(1, (1 << 29) // slot_total)
    key_full, key_rows = jax.random.split(jax.random.fold_in(key, 11))
    full_dom = jax.random.randint(key_full, (), 0, dom_total)

    def one_device(device_key):
        key_a, key_b, key_c = jax.random.split(device_key, 3)
        slot_ids = jnp.arange(slot_total, dtype=jnp.int32)
        scores = jax.random.randint(key_a, (slot_total,), 0, spread_top) * slot_total + slot_ids
        scores = jnp.where(slot_ids // CAP == full_dom, (1 << 30) + slot_ids, scores)
        chosen = lax.top_k(scores, GR_DEV)[1]
        chosen = chosen[jax.random.permutation(key_b, GR_DEV)]
        target_node = jax.random.randint(key_c, (GR_DEV,), 0, M_DEV)
        return (chosen // CAP * M_DEV + target_node).astype(jnp.int32)
    device_keys = jax.random.split(key_rows, GRID // GR_DEV)
    return jax.vmap(one_device)(device_keys).reshape(GRID)


def draw_nbr_blocks(key, part):
    window_span = BLOCKS_DEV + 2 * HB
    slot_ids = jnp.arange(window_span, dtype=jnp.int32)

    def one_block(block_id, block_key):
        device_id = block_id // BLOCKS_DEV
        own_slot = block_id - device_id * BLOCKS_DEV + HB
        scores = jax.random.randint(block_key, (window_span,), 0, 1 << 16) * window_span + slot_ids
        scores = jnp.where(slot_ids == own_slot, 1 << 30, scores)
        chosen = lax.top_k(scores, NBLK)[1]
        return ((device_id * BLOCKS_DEV - HB + chosen) % BLOCKS).astype(jnp.int32)
    block_keys = jax.random.split(jax.random.fold_in(key, 7), BLOCKS)
    return jax.vmap(one_block)(jnp.arange(BLOCKS, dtype=jnp.int32), block_keys)


def draw_attn_bias(key, part):
    key_a = jax.random.fold_in(jax.random.fold_in(key, 5), 0)
    base_bias = jax.random.uniform(key_a, (HEADS, NBLK, MESH), jnp.float32, -2.0, 2.0)
    return base_bias


def steps_of(stream_key, extent, pieces, smallest, high):
    def one(position, shards_of):
        draws = jax.random.uniform(jax.random.fold_in(jax.random.fold_in(stream_key, 6), position), (shards_of,), jnp.float32, smallest / len(pieces), high / len(pieces))
        return jnp.repeat(jnp.exp(draws), extent[position] // shards_of).reshape((-1,) + (1,) * (len(extent) - position - 1))

    gain = one(*pieces[0])
    for cut in pieces[1:]:
        gain = gain * one(*cut)
    return gain


def normal_values(rng, extent, scale, most, cuts=(), kind=jnp.bfloat16):
    factor_of = steps_of(rng, extent, cuts, -0.22, 0.18) if cuts else 1.0
    drawn = jax.random.normal(rng, extent, jnp.float32) * scale * factor_of
    return jnp.minimum(jnp.maximum(drawn, -most), most).astype(kind)


def setup_inputs(seed: int = 0) -> dict:
    key_of = jax.random.split(jax.random.key(seed), 15)
    return {
        "grid_feat": normal_values(key_of[0], (GRID, F_IN), 1.0, 6.0, ((0, 32),)),
        "grid_target": draw_grid_target(jax.random.fold_in(key_of[14], 71), 0),
        "enc_w1": normal_values(key_of[2], (F_IN, D), F_IN ** -0.5, 0.375),
        "enc_b1": normal_values(key_of[3], (D,), 0.5, 3.0, (), jnp.float32),
        "enc_w2": normal_values(key_of[4], (D, D), D ** -0.5, 0.25),
        "enc_gain": jnp.clip(1.0 + 0.15 * jax.random.normal(key_of[5], (D,), jnp.float32), 0.25, 1.75),
        "mesh_embed": normal_values(key_of[6], (MESH, D), 1.0, 6.0, ((0, 8), (1, 4))),
        "nbr_blocks": draw_nbr_blocks(jax.random.fold_in(key_of[14], 71), 0),
        "attn_bias": draw_attn_bias(jax.random.fold_in(key_of[14], 71), 0),
        "ln_gain": jnp.clip(1.0 + 0.15 * jax.random.normal(key_of[9], (LAYERS, 2, D), jnp.float32), 0.25, 1.75),
        "qkv_w": normal_values(key_of[10], (LAYERS, 3, D, D), D ** -0.5, 0.25, ((3, 4),)),
        "out_w": normal_values(key_of[11], (LAYERS, D, D), D ** -0.5, 0.25, ((1, 4),)),
        "up_w": normal_values(key_of[12], (LAYERS, D, FF), D ** -0.5, 0.25, ((2, 4),)),
        "down_w": normal_values(key_of[13], (LAYERS, FF, D), FF ** -0.5, 0.125, ((1, 4),)),
    }


EPS = 1e-05

def normalize(values, gain_vector):
    values = values.astype(jnp.float32)
    row_mean = lax.optimization_barrier(jnp.mean(values, axis=-1, keepdims=True))
    centered = values - row_mean
    variance = lax.optimization_barrier(jnp.mean(centered * centered, axis=-1, keepdims=True))
    return centered * lax.rsqrt(variance + EPS) * gain_vector

def encode(features, enc_w1, enc_b1, enc_w2, enc_gain):
    first = jnp.dot(features, enc_w1, preferred_element_type=jnp.float32) + enc_b1
    first = jax.nn.silu(first).astype(jnp.bfloat16)
    second = jnp.dot(first, enc_w2, preferred_element_type=jnp.float32)
    return normalize(second, enc_gain).astype(jnp.bfloat16)

def attend(queries, key_rows, value_rows, nbr_blocks, attn_bias):
    query_blocks = queries.reshape(N_DOM, BLOCKS_DEV, BLK, HEADS, HEAD_DIM)
    key_blocks = key_rows.reshape(BLOCKS, BLK, HEADS, HEAD_DIM)
    value_blocks = value_rows.reshape(BLOCKS, BLK, HEADS, HEAD_DIM)
    block_lists = nbr_blocks.reshape(N_DOM, BLOCKS_DEV, NBLK)
    bias_rows = jnp.transpose(attn_bias.reshape(HEADS, NBLK, N_DOM, BLOCKS_DEV, BLK), (2, 3, 0, 4, 1))

    def one_group(block_item):
        group_query, group_lists, group_bias = block_item
        group_keys = key_blocks[group_lists].reshape(BLOCKS_DEV, NBLK * BLK, HEADS, HEAD_DIM).astype(jnp.float32)
        group_values = value_blocks[group_lists].reshape(BLOCKS_DEV, NBLK * BLK, HEADS, HEAD_DIM).astype(jnp.float32)
        scores = jnp.einsum('tqhe,tkhe->thqk', group_query.astype(jnp.float32), group_keys) * HEAD_DIM ** (-0.5)
        scores = scores.reshape(BLOCKS_DEV, HEADS, BLK, NBLK, BLK) + group_bias[..., None]
        row_max = lax.optimization_barrier(jnp.max(scores, axis=(3, 4), keepdims=True))
        exponent = jnp.exp(scores - row_max)
        weights = (exponent / lax.optimization_barrier(jnp.sum(exponent, axis=(3, 4), keepdims=True))).astype(jnp.bfloat16)
        weights = weights.reshape(BLOCKS_DEV, HEADS, BLK, NBLK * BLK).astype(jnp.float32)
        attended = jnp.einsum('thqk,tkhe->tqhe', weights, group_values)
        return attended.astype(jnp.bfloat16).reshape(BLOCKS_DEV * BLK, HEADS * HEAD_DIM)
    return lax.map(one_group, (query_blocks, block_lists, bias_rows)).reshape(MESH, D)

def reference(grid_feat, grid_target, enc_w1, enc_b1, enc_w2, enc_gain, mesh_embed, nbr_blocks, attn_bias, ln_gain, qkv_w, out_w, up_w, down_w):
    features = grid_feat.reshape(GRID // GR_DEV, GR_DEV, F_IN)
    targets = grid_target.reshape(GRID // GR_DEV, GR_DEV)

    def add_block(running, block_item):
        message = encode(block_item[0], enc_w1, enc_b1, enc_w2, enc_gain)
        return (running.at[block_item[1]].add(message.astype(jnp.float32)), None)
    gathered, _ = lax.scan(add_block, jnp.zeros((MESH, D), jnp.float32), (features, targets))
    stream = (mesh_embed.astype(jnp.float32) + gathered).astype(jnp.bfloat16)
    for layer_index in range(LAYERS):
        normed = normalize(stream, ln_gain[layer_index, 0]).astype(jnp.bfloat16)
        queries = jnp.dot(normed, qkv_w[layer_index, 0], preferred_element_type=jnp.float32).astype(jnp.bfloat16)
        key_rows = jnp.dot(normed, qkv_w[layer_index, 1], preferred_element_type=jnp.float32).astype(jnp.bfloat16)
        value_rows = jnp.dot(normed, qkv_w[layer_index, 2], preferred_element_type=jnp.float32).astype(jnp.bfloat16)
        attended = attend(queries, key_rows, value_rows, nbr_blocks, attn_bias)
        stream = (stream.astype(jnp.float32) + jnp.dot(attended, out_w[layer_index], preferred_element_type=jnp.float32)).astype(jnp.bfloat16)
        normed = normalize(stream, ln_gain[layer_index, 1]).astype(jnp.bfloat16)
        hidden = jax.nn.silu(jnp.dot(normed, up_w[layer_index], preferred_element_type=jnp.float32)).astype(jnp.bfloat16)
        stream = (stream.astype(jnp.float32) + jnp.dot(hidden, down_w[layer_index], preferred_element_type=jnp.float32)).astype(jnp.bfloat16)
    return stream
```

```python
import functools

import jax
import jax.numpy as jnp
from jax import lax
from jax.experimental import pallas as pl
from jax.experimental.pallas import tpu as pltpu
from jax.sharding import PartitionSpec as P

HEAD_DIM = 64
BLK = 64
NBLK = 16
HB = 4
EPS = 1e-05
F32 = jnp.float32
BF16 = jnp.bfloat16
MESH = pl.DeviceIdType.MESH


def normalize(values, gain_row):
    row_mean = jnp.mean(values, axis=-1, keepdims=True)
    centered = values - row_mean
    variance = jnp.mean(centered * centered, axis=-1, keepdims=True)
    return centered * lax.rsqrt(variance + EPS) * gain_row


def silu(v):
    return v / (1.0 + jnp.exp(-v))


def mm(a, b):
    return jnp.dot(a, b, preferred_element_type=F32)


def mega(
    n_dom,
    n_mp,
    layers,
    slots,
    feat,
    target,
    w1,
    b1,
    w2,
    egain,
    embed,
    bias,
    ln_gain,
    qkv_w,
    out_w,
    up_w,
    down_w,
    result,
    sbuf,
    sland,
    rbuf,
    rland,
    acc,
    psend,
    precv,
    xrow,
    nrm,
    kv0,
    kv1,
    qs,
    att,
    arecv,
    gout,
    gup,
    gdown,
    d_send,
    d_recv,
    p_send,
    p_recv,
    ag_send,
    ag_recv,
    w_send,
    w_recv,
    h_send,
    h_recv,
    a_send,
    a_recv,
    f_send,
    f_recv,
):
    dom = lax.axis_index("dom")
    m = lax.axis_index("mp")
    rows = feat.shape[0]
    cap = sbuf.shape[1]
    nodes = embed.shape[0]
    cols = embed.shape[1]
    quarter = nodes // n_mp
    qblk = quarter // BLK
    heads = cols // HEAD_DIM
    local_blocks = nodes // BLK
    peers = [m + 1 - 2 * (m % 2), (m + 2) % 4, 3 - m]

    def dev(d, p):
        return (d, p)

    barrier = pltpu.get_barrier_semaphore()
    for k in range(1, n_dom):
        pl.semaphore_signal(barrier, inc=1, device_id=dev((dom + k) % n_dom, m), device_id_type=MESH)
    for p in peers:
        pl.semaphore_signal(barrier, inc=1, device_id=dev(dom, p), device_id_type=MESH)

    owner = target[...] // nodes
    node = target[...] % nodes
    row_e = lax.broadcasted_iota(jnp.int32, (n_dom, rows), 0)
    member = (row_e == owner).astype(F32)
    before = (
        lax.broadcasted_iota(jnp.int32, (rows, rows), 0)
        < lax.broadcasted_iota(jnp.int32, (rows, rows), 1)
    ).astype(F32).astype(BF16)
    count = mm(member.astype(BF16), before)
    rank = jnp.sum(count * member, axis=0, keepdims=True).astype(jnp.int32)
    slot = owner * cap + rank
    hi = (node // 32).astype(F32)
    lo = (node % 32).astype(F32)
    pick = lax.broadcasted_iota(jnp.int32, (16, rows), 0)
    parts = jnp.where(
        pick == 0, hi, jnp.where(pick == 1, lo, jnp.where(pick == 2, 1.0, 0.0))
    ).astype(BF16)
    features = feat[...]

    def outgoing(k):
        e = (dom + k) % n_dom
        here = (
            lax.broadcasted_iota(jnp.int32, (cap, rows), 0) == slot - e * cap
        ).astype(F32).astype(BF16)
        sbuf[k] = mm(here, features).astype(BF16)
        where_to = lax.dot_general(parts, here, (((1,), (1,)), ((), ())), preferred_element_type=F32)
        landed = where_to[0:1] * 32.0 + where_to[1:2]
        landed = jnp.where(where_to[2:3] > 0.5, landed, -1.0).astype(jnp.int32)
        sland[k] = jnp.broadcast_to(landed, (8, cap))

    def d_copies(k):
        target_dev = dev((dom + k) % n_dom, m)
        return (
            pltpu.make_async_remote_copy(
                sbuf.at[k], rbuf.at[k], d_send.at[0, k], d_recv.at[0, k],
                device_id=target_dev, device_id_type=MESH,
            ),
            pltpu.make_async_remote_copy(
                sland.at[k], rland.at[k], d_send.at[1, k], d_recv.at[1, k],
                device_id=target_dev, device_id_type=MESH,
            ),
        )

    order = sorted(range(1, n_dom), key=lambda k: -min(k, n_dom - k))
    outgoing(order[0])
    pl.semaphore_wait(barrier, n_dom - 1 + len(peers))
    started = {}

    def w_copies(layer, hop):
        out = []
        for i, (own, got) in enumerate(((out_w, gout), (up_w, gup), (down_w, gdown))):
            if hop < 2:
                src = own.at[layer]
                p = peers[hop]
            else:
                src = got.at[layer, 1]
                p = peers[0]
            out.append(
                pltpu.make_async_remote_copy(
                    src, got.at[layer, hop], w_send.at[layer, hop, i], w_recv.at[layer, hop, i],
                    device_id=dev(dom, p), device_id_type=MESH,
                )
            )
        return out

    wc = {(l, h): w_copies(l, h) for l in range(layers) for h in range(3)}

    def start_all(copies):
        for c in copies:
            c.start()

    for n, k in enumerate(order):
        if n:
            outgoing(k)
        started[k] = d_copies(k)
        start_all(started[k])
    start_all(wc[0, 1])
    start_all(wc[0, 0])
    outgoing(0)

    def consume(buf, land, first):
        v = mm(buf, w1[...]) + b1[...]
        message = normalize(mm(silu(v).astype(BF16), w2[...]), egain[...]).astype(BF16)
        scatter = (
            lax.broadcasted_iota(jnp.int32, (nodes, cap), 0) == land[0:1]
        ).astype(F32).astype(BF16)
        if first:
            acc[...] = mm(scatter, message)
        else:
            acc[...] += mm(scatter, message)

    consume(sbuf[0], sland[0], True)
    mine = pl.ds(pl.multiple_of(m * cols, cols), cols)
    acc[:, mine] += embed[...].astype(F32)
    for k in reversed(order):
        for c in started[k]:
            c.wait_recv()
        consume(rbuf[k], rland[k], False)

    def rows_of(p):
        return pl.ds(pl.multiple_of(p * quarter, quarter), quarter)

    pc = []
    for r in (2, 1, 0):
        psend[r] = acc[rows_of(peers[r]), :].astype(BF16)
        c = pltpu.make_async_remote_copy(
            psend.at[r], precv.at[r], p_send.at[r], p_recv.at[r],
            device_id=dev(dom, peers[r]), device_id_type=MESH,
        )
        c.start()
        pc.append(c)
    total = acc[rows_of(m), :]
    for c in reversed(pc):
        c.wait_recv()
    for r in range(3):
        total = total + precv[r].astype(F32)
    xrow[...] = total.astype(BF16)

    lane = lax.broadcasted_iota(jnp.int32, (BLK, cols), 1) // HEAD_DIM
    pending = []
    for layer in range(layers):
        kv = (kv0, kv1)[layer]
        nrm[layer, 3] = normalize(xrow[...].astype(F32), ln_gain[2 * layer : 2 * layer + 1, :]).astype(BF16)
        ag = []
        for r in range(3):
            c = pltpu.make_async_remote_copy(
                nrm.at[layer, 3], nrm.at[layer, r], ag_send.at[layer, r], ag_recv.at[layer, r],
                device_id=dev(dom, peers[r]), device_id_type=MESH,
            )
            ag.append(c)
        for r in (2, 1, 0):
            ag[r].start()
        if layer + 1 < layers:
            start_all(wc[layer + 1, 1])
            start_all(wc[layer + 1, 0])

        def project(r, p):
            block = nrm[layer, r]
            q = mm(block, qkv_w[layer, 0]).astype(BF16).astype(F32) * HEAD_DIM ** (-0.5)
            qs[layer, rows_of(p), :] = q.astype(BF16)
            spot = pl.ds(HB + p * qblk, qblk)
            kv[spot, :, 0:cols] = mm(block, qkv_w[layer, 1]).astype(BF16).reshape(qblk, BLK, cols)
            kv[spot, :, cols : 2 * cols] = (
                mm(block, qkv_w[layer, 2]).astype(BF16).reshape(qblk, BLK, cols)
            )

        project(3, m)
        for r in range(3):
            ag[r].wait_recv()
            project(r, peers[r])
        halo = [
            pltpu.make_async_remote_copy(
                kv.at[pl.ds(HB, HB)], kv.at[pl.ds(HB + local_blocks, HB)],
                h_send.at[layer, 0], h_recv.at[layer, 0],
                device_id=dev((dom + n_dom - 1) % n_dom, m), device_id_type=MESH,
            ),
            pltpu.make_async_remote_copy(
                kv.at[pl.ds(local_blocks, HB)], kv.at[pl.ds(0, HB)],
                h_send.at[layer, 1], h_recv.at[layer, 1],
                device_id=dev((dom + 1) % n_dom, m), device_id_type=MESH,
            ),
        ]
        start_all(halo)
        for c in wc[layer, 1]:
            c.wait_recv()
        start_all(wc[layer, 2])
        for c in halo:
            c.wait_recv()

        def attend(p):
            def body(i, carry):
                b = p * qblk + i
                span = pl.ds(pl.multiple_of(b * BLK, BLK), BLK)
                q = qs[layer, span, :]
                qbd = jnp.concatenate(
                    [jnp.where(lane == h, q.astype(F32), 0.0) for h in range(heads)], axis=0
                ).astype(BF16)
                picked = [kv[slots[b * NBLK + t]] for t in range(NBLK)]
                keys = jnp.concatenate([x[:, 0:cols] for x in picked], axis=0)
                values = jnp.concatenate([x[:, cols : 2 * cols] for x in picked], axis=0)
                s = lax.dot_general(keys, qbd, (((1,), (1,)), ((), ())), preferred_element_type=F32)
                s = s.reshape(NBLK, BLK, heads * BLK) + bias[b][:, None, :]
                s = s.reshape(NBLK * BLK, heads * BLK)
                e = jnp.exp(s - jnp.max(s, axis=0, keepdims=True))
                w = (e * (1.0 / jnp.sum(e, axis=0, keepdims=True))).astype(BF16)
                o = lax.dot_general(w, values, (((0,), (0,)), ((), ())), preferred_element_type=F32)
                merged = o[0:BLK]
                for h in range(1, heads):
                    merged = jnp.where(lane == h, o[h * BLK : (h + 1) * BLK], merged)
                att[layer, span, :] = merged.astype(BF16)
                return carry

            lax.fori_loop(0, qblk, body, 0)

        ac = []
        for r in (2, 1, 0):
            attend(peers[r])
            c = pltpu.make_async_remote_copy(
                att.at[layer, rows_of(peers[r])], arecv.at[layer, r],
                a_send.at[layer, r], a_recv.at[layer, r],
                device_id=dev(dom, peers[r]), device_id_type=MESH,
            )
            c.start()
            ac.append(c)
        attend(m)
        for c in wc[layer, 0] + wc[layer, 2]:
            c.wait_recv()
        y = xrow[...].astype(F32) + mm(att[layer, rows_of(m), :], out_w[layer])
        for c in ac:
            c.wait_recv()
        for r in range(3):
            y = y + mm(arecv[layer, r], gout[layer, r])
        x1 = y.astype(BF16).astype(F32)
        n2 = normalize(x1, ln_gain[2 * layer + 1 : 2 * layer + 2, :]).astype(BF16)
        total = x1 + mm(silu(mm(n2, up_w[layer])).astype(BF16), down_w[layer])
        for r in range(3):
            total = total + mm(silu(mm(n2, gup[layer, r])).astype(BF16), gdown[layer, r])
        xrow[...] = total.astype(BF16)
        pending += ag + halo + ac

    fc = []
    for r in range(3):
        c = pltpu.make_async_remote_copy(
            xrow.at[:, pl.ds(pl.multiple_of(peers[r] * cols, cols), cols)],
            result.at[rows_of(m), :],
            f_send.at[r], f_recv.at[r],
            device_id=dev(dom, peers[r]), device_id_type=MESH,
        )
        c.start()
        fc.append(c)
    result[rows_of(m), :] = xrow[:, mine]
    for k in order:
        for c in started[k]:
            c.wait_send()
    for c in pc + pending:
        c.wait_send()
    for key in wc:
        for c in wc[key]:
            c.wait_send()
    for c in fc:
        c.wait()


def shards(
    grid_feat,
    grid_target,
    enc_w1,
    enc_b1,
    enc_w2,
    enc_gain,
    mesh_embed,
    nbr_blocks,
    attn_bias,
    ln_gain,
    qkv_w,
    out_w,
    up_w,
    down_w,
):
    n_dom = lax.axis_size("dom")
    n_mp = lax.axis_size("mp")
    rows, f_in = grid_feat.shape
    width = enc_w2.shape[1]
    cols = width // n_mp
    nodes = mesh_embed.shape[0]
    local_blocks = nodes // BLK
    heads = cols // HEAD_DIM
    layers = ln_gain.shape[0]
    cap = 2 * rows // n_dom
    quarter = nodes // n_mp
    ff = up_w.shape[2]
    window_start = lax.axis_index("dom") * local_blocks - HB
    slots = ((nbr_blocks - window_start) % (local_blocks * n_dom)).reshape(-1)
    bias = jnp.transpose(
        attn_bias.reshape(heads, NBLK, local_blocks, BLK), (2, 1, 0, 3)
    ).reshape(local_blocks, NBLK, heads * BLK)
    vmem = pl.BlockSpec(memory_space=pltpu.VMEM)
    dma = pltpu.SemaphoreType.DMA
    window = local_blocks + 2 * HB
    return pl.pallas_call(
        functools.partial(mega, n_dom, n_mp, layers),
        out_shape=jax.ShapeDtypeStruct((nodes, cols), BF16),
        in_specs=[pl.BlockSpec(memory_space=pltpu.SMEM)] + [vmem] * 13,
        out_specs=vmem,
        scratch_shapes=[
            pltpu.VMEM((n_dom, cap, f_in), BF16),
            pltpu.VMEM((n_dom, 8, cap), jnp.int32),
            pltpu.VMEM((n_dom, cap, f_in), BF16),
            pltpu.VMEM((n_dom, 8, cap), jnp.int32),
            pltpu.VMEM((nodes, width), F32),
            pltpu.VMEM((3, quarter, width), BF16),
            pltpu.VMEM((3, quarter, width), BF16),
            pltpu.VMEM((quarter, width), BF16),
            pltpu.VMEM((layers, 4, quarter, width), BF16),
            pltpu.VMEM((window, BLK, 2 * cols), BF16),
            pltpu.VMEM((window, BLK, 2 * cols), BF16),
            pltpu.VMEM((layers, nodes, cols), BF16),
            pltpu.VMEM((layers, nodes, cols), BF16),
            pltpu.VMEM((layers, 3, quarter, cols), BF16),
            pltpu.VMEM((layers, 3, cols, width), BF16),
            pltpu.VMEM((layers, 3, width, ff), BF16),
            pltpu.VMEM((layers, 3, ff, width), BF16),
            dma((2, n_dom)),
            dma((2, n_dom)),
            dma((3,)),
            dma((3,)),
            dma((layers, 3)),
            dma((layers, 3)),
            dma((layers, 3, 3)),
            dma((layers, 3, 3)),
            dma((layers, 2)),
            dma((layers, 2)),
            dma((layers, 3)),
            dma((layers, 3)),
            dma((3,)),
            dma((3,)),
        ],
        compiler_params=pltpu.CompilerParams(
            collective_id=0, has_side_effects=True, vmem_limit_bytes=60 * 1024 * 1024
        ),
    )(
        slots,
        grid_feat,
        grid_target.reshape(1, rows),
        enc_w1,
        enc_b1.reshape(1, width),
        enc_w2,
        enc_gain.reshape(1, width),
        mesh_embed,
        bias,
        ln_gain.reshape(2 * layers, width),
        qkv_w,
        out_w,
        up_w,
        down_w,
    )


def solution(mesh):
    placed = (
        P(("dom", "mp"), None),
        P(("dom", "mp")),
        P(),
        P(),
        P(),
        P(),
        P("dom", "mp"),
        P("dom", None),
        P("mp", None, "dom"),
        P(),
        P(None, None, None, "mp"),
        P(None, "mp", None),
        P(None, None, "mp"),
        P(None, "mp", None),
    )
    return jax.shard_map(
        shards, mesh=mesh, in_specs=placed, out_specs=P("dom", "mp"), check_vma=False
    )
```

```python
import functools

import jax
import jax.numpy as jnp
from jax import lax
from jax.experimental import pallas as pl
from jax.experimental.pallas import tpu as pltpu
from jax.sharding import PartitionSpec as P

HEAD_DIM = 64
BLK = 64
NBLK = 16
HB = 4
EPS = 1e-05
F32 = jnp.float32
BF16 = jnp.bfloat16
MESH = pl.DeviceIdType.MESH


def normalize(values, gain_row):
    row_mean = jnp.mean(values, axis=-1, keepdims=True)
    centered = values - row_mean
    variance = jnp.mean(centered * centered, axis=-1, keepdims=True)
    return centered * lax.rsqrt(variance + EPS) * gain_row


def silu(v):
    return v / (1.0 + jnp.exp(-v))


def mm(a, b):
    return jnp.dot(a, b, preferred_element_type=F32)


def mega(
    n_dom,
    n_mp,
    layers,
    nbr,
    feat,
    target,
    w1,
    b1,
    w2,
    egain,
    embed,
    bias_in,
    ln_gain,
    qkv_hbm,
    out_hbm,
    up_hbm,
    down_hbm,
    result,
    bias,
    qkv_w,
    sbuf,
    sland,
    rbuf,
    rland,
    acc,
    psend,
    precv,
    xrow,
    nrm,
    kv0,
    kv1,
    qs,
    att,
    arecv,
    gout,
    gup,
    gdown,
    d_send,
    d_recv,
    p_send,
    p_recv,
    ag_send,
    ag_recv,
    w_send,
    w_recv,
    h_send,
    h_recv,
    a_send,
    a_recv,
    f_send,
    f_recv,
    l_sem,
):
    dom = lax.axis_index("dom")
    m = lax.axis_index("mp")
    rows = feat.shape[0]
    cap = sbuf.shape[1]
    nodes = embed.shape[0]
    cols = embed.shape[1]
    quarter = nodes // n_mp
    qblk = quarter // BLK
    heads = cols // HEAD_DIM
    local_blocks = nodes // BLK
    peers = [m + 1 - 2 * (m % 2), (m + 2) % 4, 3 - m]

    def dev(d, p):
        return (d, p)

    barrier = pltpu.get_barrier_semaphore()
    for k in range(1, n_dom):
        pl.semaphore_signal(barrier, inc=1, device_id=dev((dom + k) % n_dom, m), device_id_type=MESH)
    for p in peers:
        pl.semaphore_signal(barrier, inc=1, device_id=dev(dom, p), device_id_type=MESH)

    owner = target[...] // nodes
    node = target[...] % nodes
    row_e = lax.broadcasted_iota(jnp.int32, (n_dom, rows), 0)
    member = (row_e == owner).astype(F32)
    before = (
        lax.broadcasted_iota(jnp.int32, (rows, rows), 0)
        < lax.broadcasted_iota(jnp.int32, (rows, rows), 1)
    ).astype(F32).astype(BF16)
    count = mm(member.astype(BF16), before)
    rank = jnp.sum(count * member, axis=0, keepdims=True).astype(jnp.int32)
    slot = owner * cap + rank
    hi = (node // 32).astype(F32)
    lo = (node % 32).astype(F32)
    pick = lax.broadcasted_iota(jnp.int32, (16, rows), 0)
    parts = jnp.where(
        pick == 0, hi, jnp.where(pick == 1, lo, jnp.where(pick == 2, 1.0, 0.0))
    ).astype(BF16)
    features = feat[...]

    def outgoing(k):
        e = (dom + k) % n_dom
        here = (
            lax.broadcasted_iota(jnp.int32, (cap, rows), 0) == slot - e * cap
        ).astype(F32).astype(BF16)
        sbuf[k] = mm(here, features).astype(BF16)
        where_to = lax.dot_general(parts, here, (((1,), (1,)), ((), ())), preferred_element_type=F32)
        landed = where_to[0:1] * 32.0 + where_to[1:2]
        landed = jnp.where(where_to[2:3] > 0.5, landed, -1.0).astype(jnp.int32)
        sland[k] = jnp.broadcast_to(landed, (8, cap))

    def d_copies(k):
        target_dev = dev((dom + k) % n_dom, m)
        return (
            pltpu.make_async_remote_copy(
                sbuf.at[k], rbuf.at[k], d_send.at[0, k], d_recv.at[0, k],
                device_id=target_dev, device_id_type=MESH,
            ),
            pltpu.make_async_remote_copy(
                sland.at[k], rland.at[k], d_send.at[1, k], d_recv.at[1, k],
                device_id=target_dev, device_id_type=MESH,
            ),
        )

    order = sorted(range(1, n_dom), key=lambda k: -min(k, n_dom - k))
    outgoing(order[0])
    pl.semaphore_wait(barrier, n_dom - 1 + len(peers))
    started = {}

    weights = ((out_hbm, gout), (up_hbm, gup), (down_hbm, gdown))
    local = [pltpu.make_async_copy(qkv_hbm, qkv_w, l_sem.at[layers, 0])]
    for layer in range(layers):
        for i, (own, got) in enumerate(weights):
            local.append(
                pltpu.make_async_copy(own.at[layer], got.at[layer, 3], l_sem.at[layer, i])
            )

    def w_copies(layer, hop):
        out = []
        for i, (own, got) in enumerate(weights):
            if hop < 2:
                src = own.at[layer]
                p = peers[hop]
            else:
                src = got.at[layer, 1]
                p = peers[0]
            out.append(
                pltpu.make_async_remote_copy(
                    src, got.at[layer, hop], w_send.at[layer, hop, i], w_recv.at[layer, hop, i],
                    device_id=dev(dom, p), device_id_type=MESH,
                )
            )
        return out

    wc = {(l, h): w_copies(l, h) for l in range(layers) for h in range(3)}

    def start_all(copies):
        for c in copies:
            c.start()

    for n, k in enumerate(order):
        if n:
            outgoing(k)
        started[k] = d_copies(k)
        start_all(started[k])
    start_all(wc[0, 1])
    start_all(wc[0, 0])
    start_all(local)
    outgoing(0)
    for b in range(local_blocks):
        bias[b] = jnp.concatenate(
            [bias_in[h, :, b * BLK : (b + 1) * BLK] for h in range(heads)], axis=1
        )

    def consume(buf, land, first):
        v = mm(buf, w1[...]) + b1[...]
        message = normalize(mm(silu(v).astype(BF16), w2[...]), egain[...]).astype(BF16)
        scatter = (
            lax.broadcasted_iota(jnp.int32, (nodes, cap), 0) == land[0:1]
        ).astype(F32).astype(BF16)
        if first:
            acc[...] = mm(scatter, message)
        else:
            acc[...] += mm(scatter, message)

    consume(sbuf[0], sland[0], True)
    mine = pl.ds(pl.multiple_of(m * cols, cols), cols)
    acc[:, mine] += embed[...].astype(F32)
    for k in order:
        for c in started[k]:
            c.wait_recv()
        consume(rbuf[k], rland[k], False)

    def rows_of(p):
        return pl.ds(pl.multiple_of(p * quarter, quarter), quarter)

    def p_copy(i, p):
        return pltpu.make_async_remote_copy(
            psend.at[i], precv.at[i], p_send.at[i], p_recv.at[i],
            device_id=dev(dom, p), device_id_type=MESH,
        )

    pc = [p_copy(0, peers[0]), p_copy(1, peers[0]), p_copy(2, peers[1])]
    psend[0] = acc[rows_of(peers[2]), :].astype(BF16)
    pc[0].start()
    psend[1] = acc[rows_of(peers[0]), :].astype(BF16)
    pc[1].start()
    pc[0].wait_recv()
    psend[2] = (acc[rows_of(peers[1]), :] + precv[0].astype(F32)).astype(BF16)
    pc[2].start()
    pc[1].wait_recv()
    total = acc[rows_of(m), :] + precv[1].astype(F32)
    for c in wc[0, 1]:
        c.wait_recv()
    start_all(wc[0, 2])
    for c in local:
        c.wait()
    pc[2].wait_recv()
    total = total + precv[2].astype(F32)
    xrow[...] = total.astype(BF16)

    lane = lax.broadcasted_iota(jnp.int32, (BLK, cols), 1) // HEAD_DIM
    block_count = local_blocks * n_dom

    def slot_of(b, t):
        away = nbr[b, t] - (dom * local_blocks - HB)
        away = jnp.where(away < 0, away + block_count, away)
        away = jnp.where(away >= block_count, away - block_count, away)
        return jnp.minimum(away, local_blocks + 2 * HB - 1)

    pending = []
    for layer in range(layers):
        kv = (kv0, kv1)[layer]
        nrm[layer, 3] = normalize(xrow[...].astype(F32), ln_gain[layer, 0:1, :]).astype(BF16)
        half = quarter // 2

        def ag_copy(i, src, dst, part, p):
            return pltpu.make_async_remote_copy(
                nrm.at[layer, src, part], nrm.at[layer, dst, part],
                ag_send.at[layer, i], ag_recv.at[layer, i],
                device_id=dev(dom, p), device_id_type=MESH,
            )

        halves = [pl.ds(0, half), pl.ds(half, half)]
        ag = [ag_copy(1 + i, 3, 1, halves[i], peers[1]) for i in range(2)]
        ag.append(ag_copy(0, 3, 0, pl.ds(0, quarter), peers[0]))
        relay = [ag_copy(3 + i, 1, 2, halves[i], peers[0]) for i in range(2)]
        start_all(ag)
        halo = [
            pltpu.make_async_remote_copy(
                kv.at[pl.ds(HB, HB)], kv.at[pl.ds(HB + local_blocks, HB)],
                h_send.at[layer, 0], h_recv.at[layer, 0],
                device_id=dev((dom + n_dom - 1) % n_dom, m), device_id_type=MESH,
            ),
            pltpu.make_async_remote_copy(
                kv.at[pl.ds(local_blocks, HB)], kv.at[pl.ds(0, HB)],
                h_send.at[layer, 1], h_recv.at[layer, 1],
                device_id=dev((dom + 1) % n_dom, m), device_id_type=MESH,
            ),
        ]

        def project(r, p):
            block = nrm[layer, r]
            spot = pl.ds(HB + p * qblk, qblk)
            kv[spot, :, 0:cols] = mm(block, qkv_w[layer, 1]).astype(BF16).reshape(qblk, BLK, cols)
            kv[spot, :, cols : 2 * cols] = (
                mm(block, qkv_w[layer, 2]).astype(BF16).reshape(qblk, BLK, cols)
            )

            @pl.when(p == 0)
            def _():
                halo[0].start()

            @pl.when(p == n_mp - 1)
            def _():
                halo[1].start()

        def project_q(r, p):
            q = mm(nrm[layer, r], qkv_w[layer, 0]).astype(BF16).astype(F32) * HEAD_DIM ** (-0.5)
            qs[layer, rows_of(p), :] = q.astype(BF16)

        project(3, m)
        ag[2].wait_recv()
        project(0, peers[0])
        for i in range(2):
            ag[i].wait_recv()
            relay[i].start()
        project(1, peers[1])
        for c in relay:
            c.wait_recv()
        project(2, peers[2])
        if layer + 1 < layers:
            start_all(wc[layer + 1, 1][0:2])
            start_all(wc[layer + 1, 0][0:2])
        if layer > 0:
            for c in wc[layer, 1][0:2]:
                c.wait_recv()
            start_all(wc[layer, 2][0:2])
        project_q(3, m)
        for r in range(3):
            project_q(r, peers[r])
        for c in halo:
            c.wait_recv()

        def attend(p):
            def body(i, carry):
                b = p * qblk + i
                span = pl.ds(pl.multiple_of(b * BLK, BLK), BLK)
                q = qs[layer, span, :]
                qbd = jnp.concatenate(
                    [jnp.where(lane == h, q.astype(F32), 0.0) for h in range(heads)], axis=0
                ).astype(BF16)
                picked = [kv[slot_of(b, t)] for t in range(NBLK)]
                keys = jnp.concatenate([x[:, 0:cols] for x in picked], axis=0)
                values = jnp.concatenate([x[:, cols : 2 * cols] for x in picked], axis=0)
                s = lax.dot_general(keys, qbd, (((1,), (1,)), ((), ())), preferred_element_type=F32)
                s = s.reshape(NBLK, BLK, heads * BLK) + bias[b][:, None, :]
                s = s.reshape(NBLK * BLK, heads * BLK)
                e = jnp.exp(s - jnp.max(s, axis=0, keepdims=True))
                w = (e * (1.0 / jnp.sum(e, axis=0, keepdims=True))).astype(BF16)
                o = lax.dot_general(w, values, (((0,), (0,)), ((), ())), preferred_element_type=F32)
                merged = o[0:BLK]
                for h in range(1, heads):
                    merged = jnp.where(lane == h, o[h * BLK : (h + 1) * BLK], merged)
                att[layer, span, :] = merged.astype(BF16)
                return carry

            lax.fori_loop(0, qblk, body, 0)

        ac = []
        for r in (2, 1, 0):
            attend(peers[r])
            c = pltpu.make_async_remote_copy(
                att.at[layer, rows_of(peers[r])], arecv.at[layer, r],
                a_send.at[layer, r], a_recv.at[layer, r],
                device_id=dev(dom, peers[r]), device_id_type=MESH,
            )
            c.start()
            ac.append(c)
        if layer > 0:
            for c in wc[layer, 1][2:3]:
                c.wait_recv()
            start_all(wc[layer, 2][2:3])
        attend(m)
        for c in wc[layer, 0] + wc[layer, 2]:
            c.wait_recv()
        y = xrow[...].astype(F32) + mm(att[layer, rows_of(m), :], gout[layer, 3])
        for c in ac:
            c.wait_recv()
        for r in range(3):
            y = y + mm(arecv[layer, r], gout[layer, r])
        if layer + 1 < layers:
            start_all(wc[layer + 1, 1][2:3])
            start_all(wc[layer + 1, 0][2:3])
        x1 = y.astype(BF16).astype(F32)
        n2 = normalize(x1, ln_gain[layer, 1:2, :]).astype(BF16)
        total = x1
        for r in (3, 0, 1, 2):
            total = total + mm(silu(mm(n2, gup[layer, r])).astype(BF16), gdown[layer, r])
        xrow[...] = total.astype(BF16)
        pending += ag + relay + halo + ac

    fc = []
    for r in range(3):
        c = pltpu.make_async_remote_copy(
            xrow.at[:, pl.ds(pl.multiple_of(peers[r] * cols, cols), cols)],
            result.at[rows_of(m), :],
            f_send.at[r], f_recv.at[r],
            device_id=dev(dom, peers[r]), device_id_type=MESH,
        )
        c.start()
        fc.append(c)
    result[rows_of(m), :] = xrow[:, mine]
    for k in order:
        for c in started[k]:
            c.wait_send()
    for c in pc + pending:
        c.wait_send()
    for key in wc:
        for c in wc[key]:
            c.wait_send()
    for c in fc:
        c.wait()


def shards(
    grid_feat,
    grid_target,
    enc_w1,
    enc_b1,
    enc_w2,
    enc_gain,
    mesh_embed,
    nbr_blocks,
    attn_bias,
    ln_gain,
    qkv_w,
    out_w,
    up_w,
    down_w,
):
    n_dom = lax.axis_size("dom")
    n_mp = lax.axis_size("mp")
    rows, f_in = grid_feat.shape
    width = enc_w2.shape[1]
    cols = width // n_mp
    nodes = mesh_embed.shape[0]
    local_blocks = nodes // BLK
    heads = cols // HEAD_DIM
    layers = ln_gain.shape[0]
    cap = 2 * rows // n_dom
    quarter = nodes // n_mp
    ff = up_w.shape[2]
    vmem = pl.BlockSpec(memory_space=pltpu.VMEM)
    dma = pltpu.SemaphoreType.DMA
    window = local_blocks + 2 * HB
    return pl.pallas_call(
        functools.partial(mega, n_dom, n_mp, layers),
        out_shape=jax.ShapeDtypeStruct((nodes, cols), BF16),
        in_specs=[pl.BlockSpec(memory_space=pltpu.SMEM)] + [vmem] * 9 + [pl.BlockSpec(memory_space=pl.ANY)] * 4,
        out_specs=vmem,
        scratch_shapes=[
            pltpu.VMEM((local_blocks, NBLK, heads * BLK), F32),
            pltpu.VMEM(qkv_w.shape, BF16),
            pltpu.VMEM((n_dom, cap, f_in), BF16),
            pltpu.VMEM((n_dom, 8, cap), jnp.int32),
            pltpu.VMEM((n_dom, cap, f_in), BF16),
            pltpu.VMEM((n_dom, 8, cap), jnp.int32),
            pltpu.VMEM((nodes, width), F32),
            pltpu.VMEM((3, quarter, width), BF16),
            pltpu.VMEM((3, quarter, width), BF16),
            pltpu.VMEM((quarter, width), BF16),
            pltpu.VMEM((layers, 4, quarter, width), BF16),
            pltpu.VMEM((window, BLK, 2 * cols), BF16),
            pltpu.VMEM((window, BLK, 2 * cols), BF16),
            pltpu.VMEM((layers, nodes, cols), BF16),
            pltpu.VMEM((layers, nodes, cols), BF16),
            pltpu.VMEM((layers, 3, quarter, cols), BF16),
            pltpu.VMEM((layers, 4, cols, width), BF16),
            pltpu.VMEM((layers, 4, width, ff), BF16),
            pltpu.VMEM((layers, 4, ff, width), BF16),
            dma((2, n_dom)),
            dma((2, n_dom)),
            dma((3,)),
            dma((3,)),
            dma((layers, 5)),
            dma((layers, 5)),
            dma((layers, 3, 3)),
            dma((layers, 3, 3)),
            dma((layers, 2)),
            dma((layers, 2)),
            dma((layers, 3)),
            dma((layers, 3)),
            dma((3,)),
            dma((3,)),
            dma((layers + 1, 3)),
        ],
        compiler_params=pltpu.CompilerParams(
            collective_id=0, has_side_effects=True, vmem_limit_bytes=60 * 1024 * 1024
        ),
    )(
        nbr_blocks,
        grid_feat,
        grid_target.reshape(1, rows),
        enc_w1,
        enc_b1.reshape(1, width),
        enc_w2,
        enc_gain.reshape(1, width),
        mesh_embed,
        attn_bias,
        ln_gain,
        qkv_w,
        out_w,
        up_w,
        down_w,
    )


def solution(mesh):
    placed = (
        P(("dom", "mp"), None),
        P(("dom", "mp")),
        P(),
        P(),
        P(),
        P(),
        P("dom", "mp"),
        P("dom", None),
        P("mp", None, "dom"),
        P(),
        P(None, None, None, "mp"),
        P(None, "mp", None),
        P(None, None, "mp"),
        P(None, "mp", None),
    )
    return jax.shard_map(
        shards, mesh=mesh, in_specs=placed, out_specs=P("dom", "mp"), check_vma=False
    )
```

```python
import functools

import jax
import jax.numpy as jnp
from jax import lax
from jax.experimental import pallas as pl
from jax.experimental.pallas import tpu as pltpu
from jax.sharding import PartitionSpec as P

HEAD_DIM = 64
BLK = 64
NBLK = 16
HB = 4
EPS = 1e-05
F32 = jnp.float32
BF16 = jnp.bfloat16
MESH = pl.DeviceIdType.MESH


def normalize(values, gain_row):
    row_mean = jnp.mean(values, axis=-1, keepdims=True)
    centered = values - row_mean
    variance = jnp.mean(centered * centered, axis=-1, keepdims=True)
    return centered * lax.rsqrt(variance + EPS) * gain_row


def silu(v):
    return v / (1.0 + jnp.exp(-v))


def mm(a, b):
    return jnp.dot(a, b, preferred_element_type=F32)


def mega(
    n_dom,
    n_mp,
    layers,
    nbr,
    feat,
    target,
    w1,
    b1,
    w2,
    egain,
    embed,
    bias_in,
    ln_gain,
    qkv_hbm,
    out_hbm,
    up_hbm,
    down_hbm,
    result,
    bias,
    qkv_w,
    sbuf,
    sland,
    rbuf,
    rland,
    acc,
    psend,
    precv,
    xrow,
    nrm,
    kv0,
    kv1,
    qs,
    att,
    arecv,
    gout,
    gup,
    gdown,
    d_send,
    d_recv,
    p_send,
    p_recv,
    ag_send,
    ag_recv,
    w_send,
    w_recv,
    h_send,
    h_recv,
    a_send,
    a_recv,
    f_send,
    f_recv,
    l_sem,
):
    dom = lax.axis_index("dom")
    m = lax.axis_index("mp")
    rows = feat.shape[0]
    cap = sbuf.shape[1]
    nodes = embed.shape[0]
    cols = embed.shape[1]
    quarter = nodes // n_mp
    qblk = quarter // BLK
    heads = cols // HEAD_DIM
    local_blocks = nodes // BLK
    peers = [m + 1 - 2 * (m % 2), (m + 2) % 4, 3 - m]

    def dev(d, p):
        return (d, p)

    barrier = pltpu.get_barrier_semaphore()
    for k in range(1, n_dom):
        pl.semaphore_signal(barrier, inc=1, device_id=dev((dom + k) % n_dom, m), device_id_type=MESH)
    for p in peers:
        pl.semaphore_signal(barrier, inc=1, device_id=dev(dom, p), device_id_type=MESH)

    owner = target[...] // nodes
    node = target[...] % nodes
    row_e = lax.broadcasted_iota(jnp.int32, (n_dom, rows), 0)
    member = (row_e == owner).astype(F32)
    before = (
        lax.broadcasted_iota(jnp.int32, (rows, rows), 0)
        < lax.broadcasted_iota(jnp.int32, (rows, rows), 1)
    ).astype(F32).astype(BF16)
    count = mm(member.astype(BF16), before)
    rank = jnp.sum(count * member, axis=0, keepdims=True).astype(jnp.int32)
    slot = owner * cap + rank
    hi = (node // 32).astype(F32)
    lo = (node % 32).astype(F32)
    pick = lax.broadcasted_iota(jnp.int32, (16, rows), 0)
    parts = jnp.where(
        pick == 0, hi, jnp.where(pick == 1, lo, jnp.where(pick == 2, 1.0, 0.0))
    ).astype(BF16)
    features = feat[...]

    def outgoing(k):
        e = (dom + k) % n_dom
        here = (
            lax.broadcasted_iota(jnp.int32, (cap, rows), 0) == slot - e * cap
        ).astype(F32).astype(BF16)
        sbuf[k] = mm(here, features).astype(BF16)
        where_to = lax.dot_general(parts, here, (((1,), (1,)), ((), ())), preferred_element_type=F32)
        landed = where_to[0:1] * 32.0 + where_to[1:2]
        landed = jnp.where(where_to[2:3] > 0.5, landed, -1.0).astype(jnp.int32)
        sland[k] = jnp.broadcast_to(landed, (8, cap))

    def d_copies(k):
        target_dev = dev((dom + k) % n_dom, m)
        return (
            pltpu.make_async_remote_copy(
                sbuf.at[k], rbuf.at[k], d_send.at[0, k], d_recv.at[0, k],
                device_id=target_dev, device_id_type=MESH,
            ),
            pltpu.make_async_remote_copy(
                sland.at[k], rland.at[k], d_send.at[1, k], d_recv.at[1, k],
                device_id=target_dev, device_id_type=MESH,
            ),
        )

    order = sorted(range(1, n_dom), key=lambda k: -min(k, n_dom - k))
    outgoing(order[0])
    pl.semaphore_wait(barrier, n_dom - 1 + len(peers))
    started = {}

    weights = ((out_hbm, gout), (up_hbm, gup), (down_hbm, gdown))
    local = [pltpu.make_async_copy(qkv_hbm, qkv_w, l_sem.at[layers, 0])]
    for layer in range(layers):
        for i, (own, got) in enumerate(weights):
            local.append(
                pltpu.make_async_copy(own.at[layer], got.at[layer, 3], l_sem.at[layer, i])
            )

    def w_copies(layer, hop):
        out = []
        for i, (own, got) in enumerate(weights):
            if hop < 2:
                src = own.at[layer]
                p = peers[hop]
            else:
                src = got.at[layer, 1]
                p = peers[0]
            out.append(
                pltpu.make_async_remote_copy(
                    src, got.at[layer, hop], w_send.at[layer, hop, i], w_recv.at[layer, hop, i],
                    device_id=dev(dom, p), device_id_type=MESH,
                )
            )
        return out

    wc = {(l, h): w_copies(l, h) for l in range(layers) for h in range(3)}

    def start_all(copies):
        for c in copies:
            c.start()

    for n, k in enumerate(order):
        if n:
            outgoing(k)
        started[k] = d_copies(k)
        start_all(started[k])
    start_all(wc[0, 1])
    start_all(wc[0, 0])
    start_all(local)
    outgoing(0)
    for b in range(local_blocks):
        bias[b] = jnp.concatenate(
            [bias_in[h, :, b * BLK : (b + 1) * BLK] for h in range(heads)], axis=1
        )

    def consume(buf, land, first):
        v = mm(buf, w1[...]) + b1[...]
        message = normalize(mm(silu(v).astype(BF16), w2[...]), egain[...]).astype(BF16)
        scatter = (
            lax.broadcasted_iota(jnp.int32, (nodes, cap), 0) == land[0:1]
        ).astype(F32).astype(BF16)
        if first:
            acc[...] = mm(scatter, message)
        else:
            acc[...] += mm(scatter, message)

    consume(sbuf[0], sland[0], True)
    mine = pl.ds(pl.multiple_of(m * cols, cols), cols)
    acc[:, mine] += embed[...].astype(F32)
    for k in order:
        for c in started[k]:
            c.wait_recv()
        consume(rbuf[k], rland[k], False)

    def rows_of(p):
        return pl.ds(pl.multiple_of(p * quarter, quarter), quarter)

    def p_copy(i, p):
        return pltpu.make_async_remote_copy(
            psend.at[i], precv.at[i], p_send.at[i], p_recv.at[i],
            device_id=dev(dom, p), device_id_type=MESH,
        )

    pc = [p_copy(0, peers[0]), p_copy(1, peers[0]), p_copy(2, peers[1])]
    psend[0] = acc[rows_of(peers[2]), :].astype(BF16)
    pc[0].start()
    psend[1] = acc[rows_of(peers[0]), :].astype(BF16)
    pc[1].start()
    pc[0].wait_recv()
    psend[2] = (acc[rows_of(peers[1]), :] + precv[0].astype(F32)).astype(BF16)
    pc[2].start()
    pc[1].wait_recv()
    total = acc[rows_of(m), :] + precv[1].astype(F32)
    for c in wc[0, 1]:
        c.wait_recv()
    start_all(wc[0, 2])
    for c in local:
        c.wait()
    pc[2].wait_recv()
    total = total + precv[2].astype(F32)
    xrow[...] = total.astype(BF16)

    lane = lax.broadcasted_iota(jnp.int32, (BLK, cols), 1) // HEAD_DIM
    block_count = local_blocks * n_dom

    def slot_of(b, t):
        away = nbr[b, t] - (dom * local_blocks - HB)
        away = jnp.where(away < 0, away + block_count, away)
        away = jnp.where(away >= block_count, away - block_count, away)
        return jnp.minimum(away, local_blocks + 2 * HB - 1)

    pending = []
    for layer in range(layers):
        kv = (kv0, kv1)[layer]
        nrm[layer, 3] = normalize(xrow[...].astype(F32), ln_gain[layer, 0:1, :]).astype(BF16)
        half = quarter // 2

        def ag_copy(i, src, dst, part, p):
            return pltpu.make_async_remote_copy(
                nrm.at[layer, src, part], nrm.at[layer, dst, part],
                ag_send.at[layer, i], ag_recv.at[layer, i],
                device_id=dev(dom, p), device_id_type=MESH,
            )

        halves = [pl.ds(0, half), pl.ds(half, half)]
        ag = [ag_copy(1 + i, 3, 1, halves[i], peers[1]) for i in range(2)]
        ag.append(ag_copy(0, 3, 0, pl.ds(0, quarter), peers[0]))
        relay = [ag_copy(3 + i, 1, 2, halves[i], peers[0]) for i in range(2)]
        start_all(ag)
        halo = [
            pltpu.make_async_remote_copy(
                kv.at[pl.ds(HB, HB)], kv.at[pl.ds(HB + local_blocks, HB)],
                h_send.at[layer, 0], h_recv.at[layer, 0],
                device_id=dev((dom + n_dom - 1) % n_dom, m), device_id_type=MESH,
            ),
            pltpu.make_async_remote_copy(
                kv.at[pl.ds(local_blocks, HB)], kv.at[pl.ds(0, HB)],
                h_send.at[layer, 1], h_recv.at[layer, 1],
                device_id=dev((dom + 1) % n_dom, m), device_id_type=MESH,
            ),
        ]

        def project(r, p):
            block = nrm[layer, r]
            spot = pl.ds(HB + p * qblk, qblk)
            kv[spot, :, 0:cols] = mm(block, qkv_w[layer, 1]).astype(BF16).reshape(qblk, BLK, cols)
            kv[spot, :, cols : 2 * cols] = (
                mm(block, qkv_w[layer, 2]).astype(BF16).reshape(qblk, BLK, cols)
            )

            @pl.when(p == 0)
            def _():
                halo[0].start()

            @pl.when(p == n_mp - 1)
            def _():
                halo[1].start()

        def project_q(r, p):
            q = mm(nrm[layer, r], qkv_w[layer, 0]).astype(BF16).astype(F32) * HEAD_DIM ** (-0.5)
            qs[layer, rows_of(p), :] = q.astype(BF16)

        project(3, m)
        ag[2].wait_recv()
        project(0, peers[0])
        for i in range(2):
            ag[i].wait_recv()
            relay[i].start()
        project(1, peers[1])
        for c in relay:
            c.wait_recv()
        project(2, peers[2])
        if layer + 1 < layers:
            start_all(wc[layer + 1, 1][0:2])
            start_all(wc[layer + 1, 0][0:2])
        if layer > 0:
            for c in wc[layer, 1][0:2]:
                c.wait_recv()
            start_all(wc[layer, 2][0:2])
        project_q(3, m)
        for r in range(3):
            project_q(r, peers[r])
        for c in halo:
            c.wait_recv()

        def attend(p):
            def body(i, carry):
                b = p * qblk + i
                span = pl.ds(pl.multiple_of(b * BLK, BLK), BLK)
                q = qs[layer, span, :]
                qbd = jnp.concatenate(
                    [jnp.where(lane == h, q.astype(F32), 0.0) for h in range(heads)], axis=0
                ).astype(BF16)
                picked = [kv[slot_of(b, t)] for t in range(NBLK)]
                keys = jnp.concatenate([x[:, 0:cols] for x in picked], axis=0)
                values = jnp.concatenate([x[:, cols : 2 * cols] for x in picked], axis=0)
                s = lax.dot_general(keys, qbd, (((1,), (1,)), ((), ())), preferred_element_type=F32)
                s = s.reshape(NBLK, BLK, heads * BLK) + bias[b][:, None, :]
                s = s.reshape(NBLK * BLK, heads * BLK)
                e = jnp.exp(s - jnp.max(s, axis=0, keepdims=True))
                w = (e * (1.0 / jnp.sum(e, axis=0, keepdims=True))).astype(BF16)
                o = lax.dot_general(w, values, (((0,), (0,)), ((), ())), preferred_element_type=F32)
                merged = o[0:BLK]
                for h in range(1, heads):
                    merged = jnp.where(lane == h, o[h * BLK : (h + 1) * BLK], merged)
                att[layer, span, :] = merged.astype(BF16)
                return carry

            lax.fori_loop(0, qblk, body, 0)

        ac = []
        for r in (2, 1, 0):
            attend(peers[r])
            c = pltpu.make_async_remote_copy(
                att.at[layer, rows_of(peers[r])], arecv.at[layer, r],
                a_send.at[layer, r], a_recv.at[layer, r],
                device_id=dev(dom, peers[r]), device_id_type=MESH,
            )
            c.start()
            ac.append(c)
        if layer > 0:
            for c in wc[layer, 1][2:3]:
                c.wait_recv()
            start_all(wc[layer, 2][2:3])
        attend(m)
        for c in wc[layer, 0][0:1] + wc[layer, 2][0:1]:
            c.wait_recv()
        y = xrow[...].astype(F32) + mm(att[layer, rows_of(m), :], gout[layer, 3])
        for c, r in zip(ac, (2, 1, 0)):
            c.wait_recv()
            y = y + mm(arecv[layer, r], gout[layer, r])
        if layer + 1 < layers:
            start_all(wc[layer + 1, 1][2:3])
            start_all(wc[layer + 1, 0][2:3])
        x1 = y.astype(BF16).astype(F32)
        n2 = normalize(x1, ln_gain[layer, 1:2, :]).astype(BF16)
        total = x1
        for r in (3, 1, 0, 2):
            if r in (0, 2):
                for c in wc[layer, r][1:3]:
                    c.wait_recv()
            total = total + mm(silu(mm(n2, gup[layer, r])).astype(BF16), gdown[layer, r])
        xrow[...] = total.astype(BF16)
        pending += ag + relay + halo + ac

    fc = []
    for r in range(3):
        c = pltpu.make_async_remote_copy(
            xrow.at[:, pl.ds(pl.multiple_of(peers[r] * cols, cols), cols)],
            result.at[rows_of(m), :],
            f_send.at[r], f_recv.at[r],
            device_id=dev(dom, peers[r]), device_id_type=MESH,
        )
        c.start()
        fc.append(c)
    result[rows_of(m), :] = xrow[:, mine]
    for k in order:
        for c in started[k]:
            c.wait_send()
    for c in pc + pending:
        c.wait_send()
    for key in wc:
        for c in wc[key]:
            c.wait_send()
    for c in fc:
        c.wait()


def shards(
    grid_feat,
    grid_target,
    enc_w1,
    enc_b1,
    enc_w2,
    enc_gain,
    mesh_embed,
    nbr_blocks,
    attn_bias,
    ln_gain,
    qkv_w,
    out_w,
    up_w,
    down_w,
):
    n_dom = lax.axis_size("dom")
    n_mp = lax.axis_size("mp")
    rows, f_in = grid_feat.shape
    width = enc_w2.shape[1]
    cols = width // n_mp
    nodes = mesh_embed.shape[0]
    local_blocks = nodes // BLK
    heads = cols // HEAD_DIM
    layers = ln_gain.shape[0]
    cap = 2 * rows // n_dom
    quarter = nodes // n_mp
    ff = up_w.shape[2]
    vmem = pl.BlockSpec(memory_space=pltpu.VMEM)
    dma = pltpu.SemaphoreType.DMA
    window = local_blocks + 2 * HB
    return pl.pallas_call(
        functools.partial(mega, n_dom, n_mp, layers),
        out_shape=jax.ShapeDtypeStruct((nodes, cols), BF16),
        in_specs=[pl.BlockSpec(memory_space=pltpu.SMEM)] + [vmem] * 9 + [pl.BlockSpec(memory_space=pl.ANY)] * 4,
        out_specs=vmem,
        scratch_shapes=[
            pltpu.VMEM((local_blocks, NBLK, heads * BLK), F32),
            pltpu.VMEM(qkv_w.shape, BF16),
            pltpu.VMEM((n_dom, cap, f_in), BF16),
            pltpu.VMEM((n_dom, 8, cap), jnp.int32),
            pltpu.VMEM((n_dom, cap, f_in), BF16),
            pltpu.VMEM((n_dom, 8, cap), jnp.int32),
            pltpu.VMEM((nodes, width), F32),
            pltpu.VMEM((3, quarter, width), BF16),
            pltpu.VMEM((3, quarter, width), BF16),
            pltpu.VMEM((quarter, width), BF16),
            pltpu.VMEM((layers, 4, quarter, width), BF16),
            pltpu.VMEM((window, BLK, 2 * cols), BF16),
            pltpu.VMEM((window, BLK, 2 * cols), BF16),
            pltpu.VMEM((layers, nodes, cols), BF16),
            pltpu.VMEM((layers, nodes, cols), BF16),
            pltpu.VMEM((layers, 3, quarter, cols), BF16),
            pltpu.VMEM((layers, 4, cols, width), BF16),
            pltpu.VMEM((layers, 4, width, ff), BF16),
            pltpu.VMEM((layers, 4, ff, width), BF16),
            dma((2, n_dom)),
            dma((2, n_dom)),
            dma((3,)),
            dma((3,)),
            dma((layers, 5)),
            dma((layers, 5)),
            dma((layers, 3, 3)),
            dma((layers, 3, 3)),
            dma((layers, 2)),
            dma((layers, 2)),
            dma((layers, 3)),
            dma((layers, 3)),
            dma((3,)),
            dma((3,)),
            dma((layers + 1, 3)),
        ],
        compiler_params=pltpu.CompilerParams(
            collective_id=0, has_side_effects=True, vmem_limit_bytes=60 * 1024 * 1024
        ),
    )(
        nbr_blocks,
        grid_feat,
        grid_target.reshape(1, rows),
        enc_w1,
        enc_b1.reshape(1, width),
        enc_w2,
        enc_gain.reshape(1, width),
        mesh_embed,
        attn_bias,
        ln_gain,
        qkv_w,
        out_w,
        up_w,
        down_w,
    )


def solution(mesh):
    placed = (
        P(("dom", "mp"), None),
        P(("dom", "mp")),
        P(),
        P(),
        P(),
        P(),
        P("dom", "mp"),
        P("dom", None),
        P("mp", None, "dom"),
        P(),
        P(None, None, None, "mp"),
        P(None, "mp", None),
        P(None, None, "mp"),
        P(None, "mp", None),
    )
    return jax.shard_map(
        shards, mesh=mesh, in_specs=placed, out_specs=P("dom", "mp"), check_vma=False
    )
```
